32 devices in a mesh: req: 8 (over z, y), grp: 4 (over x, core).
Axes of the slice: x: 2, y: 2, z: 4, core: 2. Of those that a mesh axis runs over, the one named last changes fastest.
Arguments:
- tokens: bfloat16 [128, 64, 1024], P(('req', 'grp')), may hold values from -6 to 6
- kv_pool: bfloat16 [192, 256, 2048], P('req', 'grp'), may hold values from -70 to 70
- page_table: int32 [8, 16, 6], P(None, 'grp'), may hold values from 0 to 191, as said below
- cache_lens: int32 [128], P(('req', 'grp')), may hold values from 48 to 384
- draft_lengths: int32 [8, 16], P('req'), may hold values from 32 to 64, as said below
- draft_parents: int32 [128, 64], P(('req', 'grp')), may hold values from -1 to 62, as said below
- accepted_path: int32 [128, 64], P(('req', 'grp')), may hold values from -1 to 63, as said below
- prompt_group: int32 [128], P(('req', 'grp')), may hold values from 0 to 23
- memory_kv: bfloat16 [24, 256, 2048], P(None, 'req'), may hold values from -70 to 70
- w_query: bfloat16 [1024, 1024], replicated, may hold values from -0.1875 to 0.1875
- w_key: bfloat16 [1024, 1024], replicated, may hold values from -0.1875 to 0.1875
- w_value: bfloat16 [1024, 1024], replicated, may hold values from -0.1875 to 0.1875
- w_output: bfloat16 [1024, 1024], replicated, may hold values from -0.1875 to 0.1875
- w_cross_query: bfloat16 [1024, 1024], replicated, may hold values from -0.1875 to 0.1875
- w_cross_output: bfloat16 [1024, 1024], replicated, may hold values from -0.1875 to 0.1875
- w_in: bfloat16 [1024, 4096], P(None, 'grp'), may hold values from -0.1875 to 0.1875
- w_out: bfloat16 [4096, 1024], P('grp'), may hold values from -0.09375 to 0.09375
Outputs:
- layer_out: bfloat16 [128, 64, 1024], P(('req', 'grp'))
- accepted_kv: bfloat16 [128, 64, 2048], P(('req', 'grp'))
The draws below stay inside these ranges and needn't reach their ends.
Inputs may be any that keep to these rules, and one draw needn't show every extreme that they name: For each g < 4, the entries of page_table[:, g * 4 : (g + 1) * 4, :] name every row of kv_pool exactly once. Within one row r of page_table and one such g, at most 4 entries share the same value of e // 24, and for each g some row reaches 4. `draft_lengths`: each row sums to 704 and holds 64 at least once. `draft_parents`: position 0 has parent -1; position i >= 1 has its parent in max(0, i - 4) to i - 1. `accepted_path`: row n lists in increasing order the positions on the walk along draft_parents from one live draft position of request n back to position 0, then -1 in the remaining slots.
All inputs are finite; a program needn't handle non-finite values.
Results may differ from the reference program's by a relative error of at most 0.017.
Values may be sent and summed in bfloat16 or wider, within the bound.
A program may use at most 192 MiB of HBM per device.

```python
import jax
import jax.numpy as jnp
from jax import lax

D = 1024
HEADS = 16
FF = 4096
GROUPS = 24
SRC = 256
DRAFT = 64
MIN_DRAFT = 32
PAGE = 64
REQ_DEV = 4
PAGES = 6
CTX = 384
POOL_DEV = 24
CAP = 4
GROUP_TOK = 704
REQS = 128
N_REQ = 8
N_GRP = 4


def tree_tables(key):
    slot_count = N_GRP * REQ_DEV
    extra_span = DRAFT - MIN_DRAFT
    extra_units = GROUP_TOK - slot_count * MIN_DRAFT - extra_span

    def one_row(row_key):
        full_key, unit_key = jax.random.split(row_key)
        full_slot = jax.random.randint(full_key, (), 0, slot_count)
        unit_ids = jax.random.permutation(unit_key, (slot_count - 1) * extra_span)[:extra_units]
        owner_ids = unit_ids // extra_span
        counts = jnp.sum((owner_ids[:, None] == jnp.arange(slot_count - 1)[None, :]).astype(jnp.int32), axis=0)
        slot_ids = jnp.arange(slot_count)
        other_ids = jnp.clip(slot_ids - (slot_ids > full_slot).astype(jnp.int32), 0, slot_count - 2)
        row_lengths = jnp.where(slot_ids == full_slot, DRAFT, MIN_DRAFT + counts[other_ids]).astype(jnp.int32)
        return (row_lengths, slot_ids == full_slot)
    lengths, full_marks = jax.vmap(one_row)(jax.random.split(jax.random.fold_in(key, 101), N_REQ))
    positions = jnp.arange(DRAFT, dtype=jnp.int32)
    jumps = jax.random.randint(jax.random.fold_in(key, 102), (REQS, DRAFT), 0, 4)
    parents = jnp.where(positions[None, :] == 0, -1, jnp.maximum(positions[None, :] - 1 - jumps, 0)).astype(jnp.int32)
    random_leaf = jax.random.randint(jax.random.fold_in(key, 103), (REQS,), 0, lengths.reshape(REQS)).astype(jnp.int32)
    leaf = jnp.where(full_marks.reshape(REQS), DRAFT - 1, random_leaf).astype(jnp.int32)

    def walk_step(step_index, carry):
        current, marks = carry
        upward = jnp.take_along_axis(parents, current[:, None], axis=1)[:, 0]
        current = jnp.where(current > 0, upward, 0)
        marks = marks | (positions[None, :] == current[:, None])
        return (current, marks)
    start_marks = positions[None, :] == leaf[:, None]
    current, marks = lax.fori_loop(0, DRAFT - 1, walk_step, (leaf, start_marks))
    order_keys = jnp.where(marks, positions[None, :], DRAFT + positions[None, :])
    sorted_keys = jnp.sort(order_keys, axis=1)
    path_ids = jnp.where(sorted_keys < DRAFT, sorted_keys, -1).astype(jnp.int32)
    return (lengths, parents, path_ids)


def draw_draft_lengths(key, part):
    return tree_tables(key)[0]


def draw_draft_parents(key, part):
    return tree_tables(key)[1]


def draw_accepted_path(key, part):
    return tree_tables(key)[2]


def draw_page_table(key, part):
    owners = N_REQ
    pool_pages = POOL_DEV
    capacity = CAP

    def one_column(column_key):
        keys = jax.random.split(column_key, 5)
        residues = jax.random.permutation(keys[0], owners)
        positions = jnp.arange(pool_pages)
        spread_ids = jnp.where(positions < capacity, 0, 1 + (positions - capacity) % (owners - 1))
        offsets = residues[spread_ids][jax.random.permutation(keys[1], pool_pages)]
        mixer = jax.random.permutation(keys[2], owners)
        shuffle = jax.random.permutation(keys[3], owners)
        source = mixer[(shuffle[:, None] + offsets[None, :]) % owners]

        def slot_order(index):
            return jax.random.permutation(jax.random.fold_in(keys[4], index), pool_pages)
        slot_table = jax.vmap(slot_order)(jnp.arange(owners))
        slot_ids = slot_table[source, positions[None, :]]
        return (source * pool_pages + slot_ids).reshape(owners, REQ_DEV, PAGES).astype(jnp.int32)
    tables = jax.vmap(one_column)(jax.random.split(jax.random.fold_in(key, 201), N_GRP))
    return jnp.transpose(tables, (1, 0, 2, 3)).reshape(N_REQ, N_GRP * REQ_DEV, PAGES)


def spiked_field(key, shape, key_columns, value_scale):
    base_key = jax.random.fold_in(key, 0)
    values = jax.random.truncated_normal(base_key, -6.0, 6.0, shape, jnp.float32)
    boost = jnp.ones(shape[:-1] + (1,), jnp.float32)
    column_ids = jnp.arange(shape[-1])
    column_scale = jnp.where(column_ids < key_columns, boost, value_scale)
    return (values * column_scale).astype(jnp.bfloat16)


def draw_kv_pool(key, part):
    return spiked_field(jax.random.fold_in(key, 301), (N_REQ * POOL_DEV, N_GRP * PAGE, 2 * D), D, 1.0)


def draw_memory_kv(key, part):
    return spiked_field(jax.random.fold_in(key, 302), (GROUPS, SRC, 2 * D), D, 4.0)


def set_ends(result, rng, least, largest):
    place = [jax.random.randint(jax.random.fold_in(rng, axis), (), 0, length) for axis, length in enumerate(result.shape)]
    main_axis = result.shape.index(max(result.shape))
    neighbour = place[:main_axis] + [(place[main_axis] + 1) % result.shape[main_axis]] + place[main_axis + 1:]
    return result.at[tuple(place)].set(least).at[tuple(neighbour)].set(largest)


def levels(stream_key, dims, cuts, low, top_value):
    gain, own = 1.0, jax.random.fold_in(stream_key, 6)
    for position, shards_of in cuts:
        draws = jnp.exp(jax.random.uniform(jax.random.fold_in(own, position), (shards_of,), jnp.float32, low / len(cuts), top_value / len(cuts)))
        gain = gain * jnp.repeat(draws, dims[position] // shards_of).reshape([-1 if axis == position else 1 for axis in range(len(dims))])
    return gain


def bell_draw(own_key, extent, deviation, bound, shards=(), kind=jnp.bfloat16):
    values = deviation * jax.random.normal(own_key, extent, jnp.float32)
    if shards:
        values = values * levels(own_key, extent, shards, -0.22, 0.18)
    return jnp.clip(values, -bound, bound).astype(kind)


def setup_inputs(seed: int = 0) -> dict:
    streams_of = jax.random.split(jax.random.key(seed), 18)
    tokens = bell_draw(streams_of[0], (REQS, DRAFT, D), 1.0, 6.0, ((0, 32),))
    kv_pool = draw_kv_pool(jax.random.fold_in(streams_of[17], 71), 0)
    page_table = draw_page_table(jax.random.fold_in(streams_of[17], 71), 0)
    cache_lens = set_ends(jax.random.randint(streams_of[3], (REQS,), CTX // 8, CTX + 1), jax.random.fold_in(streams_of[3], 1), CTX // 8, CTX).astype(jnp.int32)
    draft_lengths = draw_draft_lengths(jax.random.fold_in(streams_of[17], 71), 0)
    draft_parents = draw_draft_parents(jax.random.fold_in(streams_of[17], 71), 0)
    accepted_path = draw_accepted_path(jax.random.fold_in(streams_of[17], 71), 0)
    prompt_group = set_ends(jax.random.randint(streams_of[7], (REQS,), 0, GROUPS), jax.random.fold_in(streams_of[7], 1), 0, GROUPS - 1).astype(jnp.int32)
    memory_kv = draw_memory_kv(jax.random.fold_in(streams_of[17], 71), 0)
    w_query = bell_draw(streams_of[9], (D, D), D ** -0.5, 0.1875)
    w_key = bell_draw(streams_of[10], (D, D), D ** -0.5, 0.1875)
    w_value = bell_draw(streams_of[11], (D, D), D ** -0.5, 0.1875)
    w_output = bell_draw(streams_of[12], (D, D), D ** -0.5, 0.1875)
    w_cross_query = bell_draw(streams_of[13], (D, D), D ** -0.5, 0.1875)
    w_cross_output = bell_draw(streams_of[14], (D, D), D ** -0.5, 0.1875)
    w_in = bell_draw(streams_of[15], (D, FF), D ** -0.5, 0.1875, ((1, 4),))
    w_out = bell_draw(streams_of[16], (FF, D), FF ** -0.5, 0.09375, ((0, 4),))
    return {"tokens": tokens, "kv_pool": kv_pool, "page_table": page_table, "cache_lens": cache_lens, "draft_lengths": draft_lengths, "draft_parents": draft_parents, "accepted_path": accepted_path, "prompt_group": prompt_group, "memory_kv": memory_kv, "w_query": w_query, "w_key": w_key, "w_value": w_value, "w_output": w_output, "w_cross_query": w_cross_query, "w_cross_output": w_cross_output, "w_in": w_in, "w_out": w_out}


EPSILON = 1e-05
NEGATIVE = -1e+30

def layer_norm(values):
    center = values - lax.optimization_barrier(jnp.mean(values, axis=-1, keepdims=True))
    spread = lax.optimization_barrier(jnp.mean(center * center, axis=-1, keepdims=True))
    return center * lax.rsqrt(spread + EPSILON)

def round_bf16(values):
    return lax.optimization_barrier(values.astype(jnp.bfloat16)).astype(jnp.float32)

def ancestors(parents):
    draft_len = parents.shape[-1]
    column_ids = jnp.arange(draft_len, dtype=jnp.int32)
    linked = (parents[:, :, None] == column_ids[None, None, :]).astype(jnp.float32)
    closure = linked + jnp.eye(draft_len, dtype=jnp.float32)[None]
    for sweep_index in range(draft_len.bit_length()):
        closure = jnp.minimum(jnp.einsum('nij,njk->nik', closure, closure, precision=lax.Precision.HIGHEST), 1.0)
    return closure

def reference(tokens, kv_pool, page_table, cache_lens, draft_lengths, draft_parents, accepted_path, prompt_group, memory_kv, w_query, w_key, w_value, w_output, w_cross_query, w_cross_output, w_in, w_out):
    draft_len = tokens.shape[1]
    model_width = tokens.shape[2]
    head_dim = model_width // HEADS
    score_scale = head_dim ** (-0.5)
    pool_blocks = kv_pool.reshape(N_REQ * POOL_DEV, N_GRP, PAGE, 2 * model_width)

    def split_heads(values):
        return values.reshape(values.shape[0], values.shape[1], HEADS, head_dim).astype(jnp.float32)

    def one_device(device):
        row_id = device // N_GRP
        col_id = device % N_GRP
        first_req = device * REQ_DEV
        zero_index = jnp.zeros((), jnp.int32)
        x_rows = lax.dynamic_slice_in_dim(tokens, first_req, REQ_DEV, 0)
        entries = lax.dynamic_slice(page_table, (row_id, col_id * REQ_DEV, zero_index), (1, REQ_DEV, PAGES)).reshape(REQ_DEV * PAGES)
        picked = jnp.take(pool_blocks, entries, axis=0)
        cache_rows = lax.dynamic_index_in_dim(picked, col_id, 1, keepdims=False).reshape(REQ_DEV, PAGES * PAGE, 2 * model_width)
        lengths = lax.dynamic_slice_in_dim(cache_lens, first_req, REQ_DEV, 0)
        counts = lax.dynamic_slice(draft_lengths, (row_id, col_id * REQ_DEV), (1, REQ_DEV))[0]
        parents = lax.dynamic_slice_in_dim(draft_parents, first_req, REQ_DEV, 0)
        path_ids = lax.dynamic_slice_in_dim(accepted_path, first_req, REQ_DEV, 0)
        groups = lax.dynamic_slice_in_dim(prompt_group, first_req, REQ_DEV, 0)
        flat_rows = x_rows.reshape(REQ_DEV * draft_len, model_width)
        query_rows = (jnp.dot(flat_rows, w_query, preferred_element_type=jnp.float32) * score_scale).astype(jnp.bfloat16)
        key_new = jnp.dot(flat_rows, w_key, preferred_element_type=jnp.float32).astype(jnp.bfloat16)
        value_new = jnp.dot(flat_rows, w_value, preferred_element_type=jnp.float32).astype(jnp.bfloat16)
        query_heads = split_heads(query_rows.reshape(REQ_DEV, draft_len, model_width))
        cache_keys = split_heads(cache_rows[:, :, :model_width])
        cache_values = split_heads(cache_rows[:, :, model_width:])
        new_keys = split_heads(key_new.reshape(REQ_DEV, draft_len, model_width))
        new_values = split_heads(value_new.reshape(REQ_DEV, draft_len, model_width))
        score_cache = jnp.einsum('nihd,nphd->nhip', query_heads, cache_keys)
        score_draft = jnp.einsum('nihd,njhd->nhij', query_heads, new_keys)
        positions = jnp.arange(cache_rows.shape[1], dtype=jnp.int32)
        score_cache = jnp.where((positions[None, :] < lengths[:, None])[:, None, None, :], score_cache, NEGATIVE)
        score_draft = jnp.where((ancestors(parents) > 0.5)[:, None, :, :], score_draft, NEGATIVE)
        top_score = jnp.maximum(lax.optimization_barrier(jnp.max(score_cache, axis=-1)), lax.optimization_barrier(jnp.max(score_draft, axis=-1)))[..., None]
        expo_cache = jnp.exp(score_cache - top_score)
        expo_draft = jnp.exp(score_draft - top_score)
        expo_total = lax.optimization_barrier(jnp.sum(expo_cache, axis=-1)) + lax.optimization_barrier(jnp.sum(expo_draft, axis=-1))
        mixed_heads = jnp.einsum('nhip,nphd->nihd', round_bf16(expo_cache), cache_values) + jnp.einsum('nhij,njhd->nihd', round_bf16(expo_draft), new_values)
        mixed_heads = mixed_heads / jnp.transpose(expo_total, (0, 2, 1))[..., None]
        self_mix = mixed_heads.reshape(REQ_DEV * draft_len, model_width).astype(jnp.bfloat16)
        first_norm = layer_norm(flat_rows.astype(jnp.float32) + jnp.dot(self_mix, w_output, preferred_element_type=jnp.float32)).astype(jnp.bfloat16)
        cross_query = (jnp.dot(first_norm, w_cross_query, preferred_element_type=jnp.float32) * score_scale).astype(jnp.bfloat16)
        cross_heads = split_heads(cross_query.reshape(REQ_DEV, draft_len, model_width))
        memory = jnp.take(memory_kv, groups, axis=0)
        memory_keys = split_heads(memory[:, :, :model_width])
        memory_values = split_heads(memory[:, :, model_width:])
        cross_scores = jnp.einsum('nihd,nphd->nhip', cross_heads, memory_keys)
        cross_top = lax.optimization_barrier(jnp.max(cross_scores, axis=-1, keepdims=True))
        cross_expo = jnp.exp(cross_scores - cross_top)
        cross_total = lax.optimization_barrier(jnp.sum(cross_expo, axis=-1))
        cross_heads_mix = jnp.einsum('nhip,nphd->nihd', round_bf16(cross_expo), memory_values)
        cross_heads_mix = cross_heads_mix / jnp.transpose(cross_total, (0, 2, 1))[..., None]
        cross_mix = cross_heads_mix.reshape(REQ_DEV * draft_len, model_width).astype(jnp.bfloat16)
        second_norm = layer_norm(first_norm.astype(jnp.float32) + jnp.dot(cross_mix, w_cross_output, preferred_element_type=jnp.float32)).astype(jnp.bfloat16)
        hidden = jax.nn.gelu(jnp.dot(second_norm, w_in, preferred_element_type=jnp.float32), approximate=False).astype(jnp.bfloat16)
        normed = layer_norm(second_norm.astype(jnp.float32) + jnp.dot(hidden, w_out, preferred_element_type=jnp.float32))
        live = (jnp.arange(draft_len, dtype=jnp.int32)[None, :] < counts[:, None]).reshape(REQ_DEV * draft_len)
        result_rows = jnp.where(live[:, None], normed, 0.0).astype(jnp.bfloat16)
        path_pick = (path_ids[:, :, None] == jnp.arange(draft_len, dtype=jnp.int32)[None, None, :]).astype(jnp.float32)
        kv_new = jnp.concatenate([key_new, value_new], axis=1).reshape(REQ_DEV, draft_len, 2 * model_width)
        accepted = jnp.einsum('nij,njc->nic', path_pick, kv_new.astype(jnp.float32)).astype(jnp.bfloat16)
        return (result_rows.reshape(REQ_DEV, draft_len, model_width), accepted)
    layer_rows, accepted_rows = lax.map(one_device, jnp.arange(N_REQ * N_GRP, dtype=jnp.int32))
    return (layer_rows.reshape(REQS, draft_len, model_width), accepted_rows.reshape(REQS, draft_len, 2 * model_width))
```

```python
import jax
import jax.numpy as jnp
from jax import lax
from jax.experimental import pallas as pl
from jax.experimental.pallas import tpu as pltpu
from jax.sharding import PartitionSpec as P

HEADS = 16
BUNDLE = 4


EPSILON = 1e-05
NEGATIVE = -1e30


def layer_norm(values):
    center = values - jnp.mean(values, axis=-1, keepdims=True)
    spread = jnp.mean(center * center, axis=-1, keepdims=True)
    return center * lax.rsqrt(spread + EPSILON)


def ancestors(parents):
    draft_len = parents.shape[-1]
    column_ids = jnp.arange(draft_len, dtype=jnp.int32)
    linked = (parents[:, :, None] == column_ids[None, None, :]).astype(jnp.float32)
    closure = linked + jnp.eye(draft_len, dtype=jnp.float32)[None]
    for sweep_index in range(draft_len.bit_length()):
        half = closure.astype(jnp.bfloat16)
        closure = jnp.minimum(
            jnp.einsum("nij,njk->nik", half, half, preferred_element_type=jnp.float32), 1.0
        )
    return closure


def copy_block(ids_ref, source_ref, out_ref):
    out_ref[...] = source_ref[...]


def take_blocks(source, ids):
    count = ids.shape[0]
    block = (1,) + source.shape[1:]
    return pl.pallas_call(
        copy_block,
        grid_spec=pltpu.PrefetchScalarGridSpec(
            num_scalar_prefetch=1,
            grid=(count,),
            in_specs=[pl.BlockSpec(block, lambda step, ids_ref: (ids_ref[step], 0, 0))],
            out_specs=pl.BlockSpec(block, lambda step, ids_ref: (step, 0, 0)),
        ),
        out_shape=jax.ShapeDtypeStruct((count,) + source.shape[1:], source.dtype),
        cost_estimate=pl.CostEstimate(
            flops=0, bytes_accessed=4 * count * source[0].size, transcendentals=0
        ),
    )(ids, source)


def attend(query, keys, values, visible):
    rows, width = query.shape
    head_dim = width // HEADS
    bundle_width = BUNDLE * head_dim
    owner_row = lax.broadcasted_iota(jnp.int32, (BUNDLE * rows, bundle_width), 0) // rows
    owner_lane = lax.broadcasted_iota(jnp.int32, (BUNDLE * rows, bundle_width), 1) // head_dim
    own = owner_row == owner_lane
    if visible is not None:
        visible = jnp.concatenate([visible] * BUNDLE, axis=0)
    mixed = []
    for bundle in range(HEADS // BUNDLE):
        lanes = slice(bundle * bundle_width, (bundle + 1) * bundle_width)
        stacked = jnp.concatenate([query[:, lanes]] * BUNDLE, axis=0)
        stacked = jnp.where(own, stacked, jnp.zeros((), stacked.dtype))
        scores = lax.dot_general(
            stacked, keys[:, lanes], (((1,), (1,)), ((), ())), preferred_element_type=jnp.float32
        )
        if visible is not None:
            scores = jnp.where(visible, scores, NEGATIVE)
        expo = jnp.exp(scores - jnp.max(scores, axis=-1, keepdims=True))
        total = jnp.sum(expo, axis=-1, keepdims=True)
        mix = jnp.dot(
            expo.astype(jnp.bfloat16), values[:, lanes], preferred_element_type=jnp.float32
        )
        mix = jnp.where(own, mix / total, 0.0)
        folded = mix[:rows]
        for part in range(1, BUNDLE):
            folded = folded + mix[part * rows : (part + 1) * rows]
        mixed.append(folded.astype(jnp.bfloat16))
    return jnp.concatenate(mixed, axis=1)


def self_kernel(ids_ref, lens_ref, query_ref, key_ref, value_ref, reach_ref, *rest):
    page_refs, out_ref = rest[:-1], rest[-1]
    request = pl.program_id(0)
    width = query_ref.shape[1]
    rows = query_ref.shape[0]
    context = sum(ref.shape[1] for ref in page_refs)
    keys = jnp.concatenate([ref[0, :, :width] for ref in page_refs] + [key_ref[...]], axis=0)
    values = jnp.concatenate([ref[0, :, width:] for ref in page_refs] + [value_ref[...]], axis=0)
    positions = lax.broadcasted_iota(jnp.int32, (rows, context), 1)
    cached = jnp.where(positions < lens_ref[request], 1.0, 0.0)
    visible = jnp.concatenate([cached, reach_ref[0]], axis=1) > 0.5
    out_ref[...] = attend(query_ref[...], keys, values, visible)


def self_attention(query, key_new, value_new, pages, page_ids, cache_lens, reach):
    req_count, draft_len, _ = reach.shape
    width = query.shape[1]
    page_count = page_ids.shape[0] // req_count
    page_block = (1,) + pages.shape[1:]
    row_spec = pl.BlockSpec((draft_len, width), lambda n, ids, lens: (n, 0))

    def page_spec(place):
        return pl.BlockSpec(page_block, lambda n, ids, lens: (ids[n * page_count + place], 0, 0))

    keys_total = page_count * pages.shape[1] + draft_len
    return pl.pallas_call(
        self_kernel,
        grid_spec=pltpu.PrefetchScalarGridSpec(
            num_scalar_prefetch=2,
            grid=(req_count,),
            in_specs=[
                row_spec,
                row_spec,
                row_spec,
                pl.BlockSpec((1, draft_len, draft_len), lambda n, ids, lens: (n, 0, 0)),
            ]
            + [page_spec(place) for place in range(page_count)],
            out_specs=row_spec,
        ),
        out_shape=jax.ShapeDtypeStruct(query.shape, jnp.bfloat16),
        cost_estimate=pl.CostEstimate(
            flops=4 * BUNDLE * query.shape[0] * keys_total * width,
            bytes_accessed=4 * req_count * keys_total * width + 8 * query.size,
            transcendentals=query.shape[0] * keys_total * HEADS,
        ),
    )(page_ids, cache_lens, query, key_new, value_new, reach, *([pages] * page_count))


def cross_kernel(query_ref, memory_ref, out_ref):
    width = query_ref.shape[1]
    positions = memory_ref.shape[0] * memory_ref.shape[2]
    keys = memory_ref[:, 0, :, :width].reshape(positions, width)
    values = memory_ref[:, 0, :, width:].reshape(positions, width)
    out_ref[...] = attend(query_ref[...], keys, values, None)


def cross_attention(query, memory):
    owners, req_count, local_src, width_both = memory.shape
    rows, width = query.shape
    draft_len = rows // req_count
    row_spec = pl.BlockSpec((draft_len, width), lambda n: (n, 0))
    return pl.pallas_call(
        cross_kernel,
        grid=(req_count,),
        in_specs=[
            row_spec,
            pl.BlockSpec((owners, 1, local_src, width_both), lambda n: (0, n, 0, 0)),
        ],
        out_specs=row_spec,
        out_shape=jax.ShapeDtypeStruct(query.shape, jnp.bfloat16),
        cost_estimate=pl.CostEstimate(
            flops=4 * BUNDLE * rows * owners * local_src * width,
            bytes_accessed=2 * memory.size + 4 * query.size,
            transcendentals=rows * owners * local_src * HEADS,
        ),
    )(query, memory)


def page_plan(page_table, pool_pages, row_index):
    owners = page_table.shape[0]
    capacity = pool_pages // owners + 1
    page_map = page_table.reshape(owners, -1)
    source = page_map // pool_pages
    slot_ids = page_map % pool_pages
    from_here = source == row_index
    send_order = jnp.cumsum(from_here.astype(jnp.int32), axis=1) - 1
    slots = jnp.arange(capacity, dtype=jnp.int32)
    placing = from_here[:, :, None] & (send_order[:, :, None] == slots[None, None, :])
    send_ids = jnp.sum(jnp.where(placing, slot_ids[:, :, None], 0), axis=1).reshape(-1)
    my_source = lax.dynamic_index_in_dim(source, row_index, 0, keepdims=False)
    page_ids = jnp.arange(page_map.shape[1], dtype=jnp.int32)
    earlier = (my_source[:, None] == my_source[None, :]) & (page_ids[None, :] < page_ids[:, None])
    page_rank = jnp.sum(earlier.astype(jnp.int32), axis=1)
    return send_ids, my_source * capacity + page_rank


def exchange(packed, owners):
    shaped = packed.reshape((owners, packed.shape[0] // owners) + packed.shape[1:])
    return lax.all_to_all(shaped, "req", split_axis=0, concat_axis=0, tiled=True)


def per_device(
    tokens,
    kv_pool,
    page_table,
    cache_lens,
    draft_lengths,
    draft_parents,
    accepted_path,
    prompt_group,
    memory_kv,
    w_query,
    w_key,
    w_value,
    w_output,
    w_cross_query,
    w_cross_output,
    w_in,
    w_out,
):
    req_count, draft_len, model_width = tokens.shape
    owners = page_table.shape[0]
    head_dim = model_width // HEADS
    scale = head_dim ** (-0.5)
    row_index = lax.axis_index("req")
    col_index = lax.axis_index("grp")
    all_groups = lax.all_gather(prompt_group, "req", axis=0, tiled=True)
    w_in_full = lax.all_gather(w_in, "grp", axis=0, tiled=False)
    w_out_full = lax.all_gather(w_out, "grp", axis=0, tiled=True)
    send_ids, page_ids = page_plan(page_table, kv_pool.shape[0], row_index)
    pages = exchange(take_blocks(kv_pool, send_ids), owners)
    pages = pages.reshape((-1,) + kv_pool.shape[1:])
    memory = exchange(take_blocks(memory_kv, all_groups), owners)

    flat_rows = tokens.reshape(req_count * draft_len, model_width)
    query_rows = (jnp.dot(flat_rows, w_query, preferred_element_type=jnp.float32) * scale).astype(
        jnp.bfloat16
    )
    key_new = jnp.dot(flat_rows, w_key, preferred_element_type=jnp.float32).astype(jnp.bfloat16)
    value_new = jnp.dot(flat_rows, w_value, preferred_element_type=jnp.float32).astype(jnp.bfloat16)
    reach = ancestors(draft_parents)
    path_pick = (
        accepted_path[:, :, None] == jnp.arange(draft_len, dtype=jnp.int32)[None, None, :]
    ).astype(jnp.bfloat16)
    accepted_kv = jnp.concatenate(
        [
            jnp.einsum(
                "nij,njc->nic",
                path_pick,
                part.reshape(req_count, draft_len, model_width),
                preferred_element_type=jnp.float32,
            ).astype(jnp.bfloat16)
            for part in (key_new, value_new)
        ],
        axis=2,
    )
    self_mix = self_attention(query_rows, key_new, value_new, pages, page_ids, cache_lens, reach)
    first_norm = layer_norm(
        flat_rows.astype(jnp.float32)
        + jnp.dot(self_mix, w_output, preferred_element_type=jnp.float32)
    ).astype(jnp.bfloat16)
    cross_query = (
        jnp.dot(first_norm, w_cross_query, preferred_element_type=jnp.float32) * scale
    ).astype(jnp.bfloat16)
    cross_mix = cross_attention(cross_query, memory)
    second_norm = layer_norm(
        first_norm.astype(jnp.float32)
        + jnp.dot(cross_mix, w_cross_output, preferred_element_type=jnp.float32)
    ).astype(jnp.bfloat16)
    summed = jnp.zeros(second_norm.shape, jnp.float32)
    hidden = [
        jax.nn.gelu(
            jnp.dot(second_norm, w_in_full[part], preferred_element_type=jnp.float32),
            approximate=False,
        ).astype(jnp.bfloat16)
        for part in range(w_in_full.shape[0])
    ]
    summed = jnp.dot(
        jnp.concatenate(hidden, axis=1), w_out_full, preferred_element_type=jnp.float32
    )
    group_lengths = draft_lengths[0]
    own_counts = lax.dynamic_slice_in_dim(group_lengths, col_index * req_count, req_count, 0)
    live = (jnp.arange(draft_len, dtype=jnp.int32)[None, :] < own_counts[:, None]).reshape(
        req_count * draft_len
    )
    normed = layer_norm(second_norm.astype(jnp.float32) + summed).astype(jnp.bfloat16)
    result_rows = jnp.where(live[:, None], normed, jnp.zeros((), jnp.bfloat16))
    return (result_rows.reshape(req_count, draft_len, model_width), accepted_kv)


def solution(mesh):
    return jax.shard_map(
        per_device,
        mesh=mesh,
        in_specs=(
            P(("req", "grp"), None, None),
            P("req", "grp", None),
            P(None, "grp", None),
            P(("req", "grp")),
            P("req", None),
            P(("req", "grp"), None),
            P(("req", "grp"), None),
            P(("req", "grp")),
            P(None, "req", None),
            P(),
            P(),
            P(),
            P(),
            P(),
            P(),
            P(None, "grp"),
            P("grp", None),
        ),
        out_specs=(P(("req", "grp"), None, None), P(("req", "grp"), None, None)),
        check_vma=False,
    )
```

```python
import functools

import jax
import jax.numpy as jnp
from jax import lax
from jax.experimental import pallas as pl
from jax.experimental.pallas import tpu as pltpu
from jax.sharding import PartitionSpec as P

HEADS = 16
BUNDLE = 4


EPSILON = 1e-05
NEGATIVE = -1e30


def layer_norm(values):
    center = values - jnp.mean(values, axis=-1, keepdims=True)
    spread = jnp.mean(center * center, axis=-1, keepdims=True)
    return center * lax.rsqrt(spread + EPSILON)


def ancestors(parents):
    draft_len = parents.shape[-1]
    column_ids = jnp.arange(draft_len, dtype=jnp.int32)
    linked = (parents[:, :, None] == column_ids[None, None, :]).astype(jnp.float32)
    closure = linked + jnp.eye(draft_len, dtype=jnp.float32)[None]
    for sweep_index in range(draft_len.bit_length()):
        half = closure.astype(jnp.bfloat16)
        closure = jnp.minimum(
            jnp.einsum("nij,njk->nik", half, half, preferred_element_type=jnp.float32), 1.0
        )
    return closure


def pack_kernel(count, ids_ref, source_ref, out_ref, sems):
    copies = [
        pltpu.make_async_copy(source_ref.at[ids_ref[slot]], out_ref.at[slot], sems.at[slot])
        for slot in range(count)
    ]
    for copy in copies:
        copy.start()
    for copy in copies:
        copy.wait()


def take_blocks(source, ids):
    count = ids.shape[0]
    return pl.pallas_call(
        functools.partial(pack_kernel, count),
        in_specs=[
            pl.BlockSpec(memory_space=pltpu.SMEM),
            pl.BlockSpec(memory_space=pl.ANY),
        ],
        out_specs=pl.BlockSpec(memory_space=pl.ANY),
        out_shape=jax.ShapeDtypeStruct((count,) + source.shape[1:], source.dtype),
        scratch_shapes=[pltpu.SemaphoreType.DMA((count,))],
        cost_estimate=pl.CostEstimate(
            flops=0, bytes_accessed=4 * count * source[0].size, transcendentals=0
        ),
    )(ids, source)


def prompt_pack_kernel(parts, slots, ids_ref, source_ref, *rest):
    out_refs, sems = rest[:parts], rest[parts]
    copies = [
        pltpu.make_async_copy(
            source_ref.at[:, ids_ref[part * slots + slot]],
            out_refs[part].at[slot],
            sems.at[part * slots + slot],
        )
        for part in range(parts)
        for slot in range(slots)
    ]
    for copy in copies:
        copy.start()
    for copy in copies:
        copy.wait()


def take_prompts(source, ids, parts):
    owners, _, rows, width = source.shape
    slots = ids.shape[0] // parts
    shape = jax.ShapeDtypeStruct((slots, owners, rows, width), source.dtype)
    return pl.pallas_call(
        functools.partial(prompt_pack_kernel, parts, slots),
        in_specs=[
            pl.BlockSpec(memory_space=pltpu.SMEM),
            pl.BlockSpec(memory_space=pl.ANY),
        ],
        out_specs=[pl.BlockSpec(memory_space=pl.ANY)] * parts,
        out_shape=[shape] * parts,
        scratch_shapes=[pltpu.SemaphoreType.DMA((parts * slots,))],
        cost_estimate=pl.CostEstimate(
            flops=0, bytes_accessed=4 * parts * shape.size, transcendentals=0
        ),
    )(ids, source)


def attend(query, keys, values, visible):
    rows, width = query.shape
    head_dim = width // HEADS
    bundle_width = BUNDLE * head_dim
    owner_row = lax.broadcasted_iota(jnp.int32, (BUNDLE * rows, bundle_width), 0) // rows
    owner_lane = lax.broadcasted_iota(jnp.int32, (BUNDLE * rows, bundle_width), 1) // head_dim
    own = owner_row == owner_lane
    if visible is not None:
        visible = jnp.concatenate([visible] * BUNDLE, axis=0)
    mixed = []
    for bundle in range(HEADS // BUNDLE):
        lanes = slice(bundle * bundle_width, (bundle + 1) * bundle_width)
        stacked = jnp.concatenate([query[:, lanes]] * BUNDLE, axis=0)
        stacked = jnp.where(own, stacked, jnp.zeros((), stacked.dtype))
        scores = lax.dot_general(
            stacked, keys[:, lanes], (((1,), (1,)), ((), ())), preferred_element_type=jnp.float32
        )
        if visible is not None:
            scores = jnp.where(visible, scores, NEGATIVE)
        expo = jnp.exp(scores - jnp.max(scores, axis=-1, keepdims=True))
        total = jnp.sum(expo, axis=-1, keepdims=True)
        mix = jnp.dot(
            expo.astype(jnp.bfloat16), values[:, lanes], preferred_element_type=jnp.float32
        )
        mix = jnp.where(own, mix / total, 0.0)
        folded = mix[:rows]
        for part in range(1, BUNDLE):
            folded = folded + mix[part * rows : (part + 1) * rows]
        mixed.append(folded.astype(jnp.bfloat16))
    return jnp.concatenate(mixed, axis=1)


def self_kernel(ids_ref, lens_ref, query_ref, key_ref, value_ref, reach_ref, *rest):
    page_refs, out_ref = rest[:-1], rest[-1]
    request = pl.program_id(0)
    width = query_ref.shape[1]
    rows = query_ref.shape[0]
    context = sum(ref.shape[1] for ref in page_refs)
    keys = jnp.concatenate([ref[0, :, :width] for ref in page_refs] + [key_ref[...]], axis=0)
    values = jnp.concatenate([ref[0, :, width:] for ref in page_refs] + [value_ref[...]], axis=0)
    positions = lax.broadcasted_iota(jnp.int32, (rows, context), 1)
    cached = jnp.where(positions < lens_ref[request], 1.0, 0.0)
    visible = jnp.concatenate([cached, reach_ref[0]], axis=1) > 0.5
    out_ref[...] = attend(query_ref[...], keys, values, visible)


def self_attention(query, key_new, value_new, pages, page_ids, cache_lens, reach):
    req_count, draft_len, _ = reach.shape
    width = query.shape[1]
    page_count = page_ids.shape[0] // req_count
    page_block = (1,) + pages.shape[1:]
    row_spec = pl.BlockSpec((draft_len, width), lambda n, ids, lens: (n, 0))

    def page_spec(place):
        return pl.BlockSpec(page_block, lambda n, ids, lens: (ids[n * page_count + place], 0, 0))

    keys_total = page_count * pages.shape[1] + draft_len
    return pl.pallas_call(
        self_kernel,
        grid_spec=pltpu.PrefetchScalarGridSpec(
            num_scalar_prefetch=2,
            grid=(req_count,),
            in_specs=[
                row_spec,
                row_spec,
                row_spec,
                pl.BlockSpec((1, draft_len, draft_len), lambda n, ids, lens: (n, 0, 0)),
            ]
            + [page_spec(place) for place in range(page_count)],
            out_specs=row_spec,
        ),
        out_shape=jax.ShapeDtypeStruct(query.shape, jnp.bfloat16),
        cost_estimate=pl.CostEstimate(
            flops=4 * BUNDLE * query.shape[0] * keys_total * width,
            bytes_accessed=4 * req_count * keys_total * width + 8 * query.size,
            transcendentals=query.shape[0] * keys_total * HEADS,
        ),
    )(page_ids, cache_lens, query, key_new, value_new, reach, *([pages] * page_count))


def cross_kernel(query_ref, *rest):
    memory_refs, out_ref = rest[:-1], rest[-1]
    width = query_ref.shape[1]

    def joined(lanes):
        return jnp.concatenate(
            [
                ref[0, block, :, lanes]
                for ref in memory_refs
                for block in range(ref.shape[1])
            ],
            axis=0,
        )

    out_ref[...] = attend(
        query_ref[...], joined(slice(0, width)), joined(slice(width, 2 * width)), None
    )


def cross_attention(query, memory_parts):
    req_count = memory_parts[0].shape[0]
    rows, width = query.shape
    draft_len = rows // req_count
    row_spec = pl.BlockSpec((draft_len, width), lambda n: (n, 0))
    memory_size = sum(part.size for part in memory_parts)
    return pl.pallas_call(
        cross_kernel,
        grid=(req_count,),
        in_specs=[row_spec]
        + [pl.BlockSpec((1,) + part.shape[1:], lambda n: (n, 0, 0, 0)) for part in memory_parts],
        out_specs=row_spec,
        out_shape=jax.ShapeDtypeStruct(query.shape, jnp.bfloat16),
        cost_estimate=pl.CostEstimate(
            flops=2 * BUNDLE * draft_len * memory_size,
            bytes_accessed=2 * memory_size + 4 * query.size,
            transcendentals=HEADS * draft_len * memory_size // (2 * width),
        ),
    )(query, *memory_parts)


def fetch_prompts(memory_kv):
    columns = lax.axis_size("grp")
    col_index = lax.axis_index("grp")
    share = memory_kv.shape[1] // columns
    quarter = lax.dynamic_slice_in_dim(memory_kv, col_index * share, share, 1)
    return lax.all_gather(quarter, "req", axis=0, tiled=False)


def trade_prompts(gathered, column_groups):
    columns = lax.axis_size("grp")
    col_index = lax.axis_index("grp")
    rolled = lax.dynamic_slice_in_dim(
        jnp.concatenate([column_groups, column_groups], axis=0), col_index, columns, 0
    )
    packed = take_prompts(gathered, rolled.reshape(-1), columns)
    arrived = [packed[0]]
    for shift in range(1, columns):
        ring = [(column, (column + shift) % columns) for column in range(columns)]
        arrived.append(lax.ppermute(packed[shift], "grp", ring))
    return arrived


def page_plan(page_table, pool_pages, row_index):
    owners = page_table.shape[0]
    capacity = pool_pages // owners + 1
    page_map = page_table.reshape(owners, -1)
    source = page_map // pool_pages
    slot_ids = page_map % pool_pages
    from_here = source == row_index
    send_order = jnp.cumsum(from_here.astype(jnp.int32), axis=1) - 1
    slots = jnp.arange(capacity, dtype=jnp.int32)
    placing = from_here[:, :, None] & (send_order[:, :, None] == slots[None, None, :])
    send_ids = jnp.sum(jnp.where(placing, slot_ids[:, :, None], 0), axis=1).reshape(-1)
    my_source = lax.dynamic_index_in_dim(source, row_index, 0, keepdims=False)
    page_ids = jnp.arange(page_map.shape[1], dtype=jnp.int32)
    earlier = (my_source[:, None] == my_source[None, :]) & (page_ids[None, :] < page_ids[:, None])
    page_rank = jnp.sum(earlier.astype(jnp.int32), axis=1)
    return send_ids, my_source * capacity + page_rank


def exchange(packed, owners):
    shaped = packed.reshape((owners, packed.shape[0] // owners) + packed.shape[1:])
    return lax.all_to_all(shaped, "req", split_axis=0, concat_axis=0, tiled=True)


def per_device(
    tokens,
    kv_pool,
    page_table,
    cache_lens,
    draft_lengths,
    draft_parents,
    accepted_path,
    prompt_group,
    memory_kv,
    w_query,
    w_key,
    w_value,
    w_output,
    w_cross_query,
    w_cross_output,
    w_in,
    w_out,
):
    req_count, draft_len, model_width = tokens.shape
    owners = page_table.shape[0]
    head_dim = model_width // HEADS
    scale = head_dim ** (-0.5)
    row_index = lax.axis_index("req")
    col_index = lax.axis_index("grp")
    send_ids, page_ids = page_plan(page_table, kv_pool.shape[0], row_index)
    shared = memory_kv.shape[1] // lax.axis_size("grp") >= 8
    if shared:
        column_groups = lax.all_gather(prompt_group, "grp", axis=0, tiled=False)
        send_ids, column_groups = lax.optimization_barrier((send_ids, column_groups))
        gathered = fetch_prompts(memory_kv)
        packed, w_in, w_out = lax.optimization_barrier(
            (take_blocks(kv_pool, send_ids), w_in, w_out)
        )
        pages = exchange(packed, owners)
        memory_parts = trade_prompts(gathered, column_groups)
    else:
        all_groups = lax.all_gather(prompt_group, "req", axis=0, tiled=True)
        pages = exchange(take_blocks(kv_pool, send_ids), owners)
        memory = exchange(take_blocks(memory_kv, all_groups), owners)
        memory_parts = [jnp.transpose(memory, (1, 0, 2, 3))]
    pages = pages.reshape((-1,) + kv_pool.shape[1:])
    w_in_full = lax.all_gather(w_in, "grp", axis=0, tiled=False)
    w_out_full = lax.all_gather(w_out, "grp", axis=0, tiled=True)

    flat_rows = tokens.reshape(req_count * draft_len, model_width)
    query_rows = (jnp.dot(flat_rows, w_query, preferred_element_type=jnp.float32) * scale).astype(
        jnp.bfloat16
    )
    key_new = jnp.dot(flat_rows, w_key, preferred_element_type=jnp.float32).astype(jnp.bfloat16)
    value_new = jnp.dot(flat_rows, w_value, preferred_element_type=jnp.float32).astype(jnp.bfloat16)
    reach = ancestors(draft_parents)
    path_pick = (
        accepted_path[:, :, None] == jnp.arange(draft_len, dtype=jnp.int32)[None, None, :]
    ).astype(jnp.bfloat16)
    accepted_kv = jnp.concatenate(
        [
            jnp.einsum(
                "nij,njc->nic",
                path_pick,
                part.reshape(req_count, draft_len, model_width),
                preferred_element_type=jnp.float32,
            ).astype(jnp.bfloat16)
            for part in (key_new, value_new)
        ],
        axis=2,
    )
    self_mix = self_attention(query_rows, key_new, value_new, pages, page_ids, cache_lens, reach)
    first_norm = layer_norm(
        flat_rows.astype(jnp.float32)
        + jnp.dot(self_mix, w_output, preferred_element_type=jnp.float32)
    ).astype(jnp.bfloat16)
    cross_query = (
        jnp.dot(first_norm, w_cross_query, preferred_element_type=jnp.float32) * scale
    ).astype(jnp.bfloat16)
    cross_mix = cross_attention(cross_query, memory_parts)
    second_norm = layer_norm(
        first_norm.astype(jnp.float32)
        + jnp.dot(cross_mix, w_cross_output, preferred_element_type=jnp.float32)
    ).astype(jnp.bfloat16)
    summed = jnp.zeros(second_norm.shape, jnp.float32)
    hidden = [
        jax.nn.gelu(
            jnp.dot(second_norm, w_in_full[part], preferred_element_type=jnp.float32),
            approximate=False,
        ).astype(jnp.bfloat16)
        for part in range(w_in_full.shape[0])
    ]
    summed = jnp.dot(
        jnp.concatenate(hidden, axis=1), w_out_full, preferred_element_type=jnp.float32
    )
    group_lengths = draft_lengths[0]
    own_counts = lax.dynamic_slice_in_dim(group_lengths, col_index * req_count, req_count, 0)
    live = (jnp.arange(draft_len, dtype=jnp.int32)[None, :] < own_counts[:, None]).reshape(
        req_count * draft_len
    )
    normed = layer_norm(second_norm.astype(jnp.float32) + summed).astype(jnp.bfloat16)
    result_rows = jnp.where(live[:, None], normed, jnp.zeros((), jnp.bfloat16))
    return (result_rows.reshape(req_count, draft_len, model_width), accepted_kv)


def solution(mesh):
    return jax.shard_map(
        per_device,
        mesh=mesh,
        in_specs=(
            P(("req", "grp"), None, None),
            P("req", "grp", None),
            P(None, "grp", None),
            P(("req", "grp")),
            P("req", None),
            P(("req", "grp"), None),
            P(("req", "grp"), None),
            P(("req", "grp")),
            P(None, "req", None),
            P(),
            P(),
            P(),
            P(),
            P(),
            P(),
            P(None, "grp"),
            P("grp", None),
        ),
        out_specs=(P(("req", "grp"), None, None), P(("req", "grp"), None, None)),
        check_vma=False,
    )
```

```python
import functools

import jax
import jax.numpy as jnp
from jax import lax
from jax.experimental import pallas as pl
from jax.experimental.pallas import tpu as pltpu
from jax.sharding import PartitionSpec as P

HEADS = 16
BUNDLE = 4


EPSILON = 1e-05
NEGATIVE = -1e30


def layer_norm(values):
    center = values - jnp.mean(values, axis=-1, keepdims=True)
    spread = jnp.mean(center * center, axis=-1, keepdims=True)
    return center * lax.rsqrt(spread + EPSILON)


def ancestors(parents):
    draft_len = parents.shape[-1]
    column_ids = jnp.arange(draft_len, dtype=jnp.int32)
    linked = (parents[:, :, None] == column_ids[None, None, :]).astype(jnp.float32)
    closure = linked + jnp.eye(draft_len, dtype=jnp.float32)[None]
    for sweep_index in range(draft_len.bit_length()):
        half = closure.astype(jnp.bfloat16)
        closure = jnp.minimum(
            jnp.einsum("nij,njk->nik", half, half, preferred_element_type=jnp.float32), 1.0
        )
    return closure


VMEM_BYTES = 24 * 1024 * 1024


def stream(sources, targets, held_ref, in_sems, out_sems):
    loads = [
        pltpu.make_async_copy(source, held_ref.at[slot], in_sems.at[slot])
        for slot, source in enumerate(sources)
    ]
    stores = [
        pltpu.make_async_copy(held_ref.at[slot], target, out_sems.at[slot])
        for slot, target in enumerate(targets)
    ]
    for load in loads:
        load.start()
    for load, store in zip(loads, stores):
        load.wait()
        store.start()
    for store in stores:
        store.wait()


def pack_kernel(count, ids_ref, source_ref, out_ref, held_ref, in_sems, out_sems):
    sources = [source_ref.at[ids_ref[slot]] for slot in range(count)]
    stream(sources, [out_ref.at[slot] for slot in range(count)], held_ref, in_sems, out_sems)


def take_blocks(source, ids):
    count = ids.shape[0]
    return pl.pallas_call(
        functools.partial(pack_kernel, count),
        in_specs=[
            pl.BlockSpec(memory_space=pltpu.SMEM),
            pl.BlockSpec(memory_space=pl.ANY),
        ],
        out_specs=pl.BlockSpec(memory_space=pl.ANY),
        out_shape=jax.ShapeDtypeStruct((count,) + source.shape[1:], source.dtype),
        scratch_shapes=[
            pltpu.VMEM((count,) + source.shape[1:], source.dtype),
            pltpu.SemaphoreType.DMA((count,)),
            pltpu.SemaphoreType.DMA((count,)),
        ],
        compiler_params=pltpu.CompilerParams(vmem_limit_bytes=VMEM_BYTES),
        cost_estimate=pl.CostEstimate(
            flops=0, bytes_accessed=4 * count * source[0].size, transcendentals=0
        ),
    )(ids, source)


def prompt_pack_kernel(parts, slots, ids_ref, source_ref, *rest):
    out_refs = rest[:parts]
    held_ref, in_sems, out_sems = rest[parts:]
    sources = [source_ref.at[:, ids_ref[place]] for place in range(parts * slots)]
    targets = [out_refs[part].at[slot] for part in range(parts) for slot in range(slots)]
    stream(sources, targets, held_ref, in_sems, out_sems)


def take_prompts(source, ids, parts):
    owners, _, rows, width = source.shape
    slots = ids.shape[0] // parts
    shape = jax.ShapeDtypeStruct((slots, owners, rows, width), source.dtype)
    return pl.pallas_call(
        functools.partial(prompt_pack_kernel, parts, slots),
        in_specs=[
            pl.BlockSpec(memory_space=pltpu.SMEM),
            pl.BlockSpec(memory_space=pl.ANY),
        ],
        out_specs=[pl.BlockSpec(memory_space=pl.ANY)] * parts,
        out_shape=[shape] * parts,
        scratch_shapes=[
            pltpu.VMEM((parts * slots,) + shape.shape[1:], source.dtype),
            pltpu.SemaphoreType.DMA((parts * slots,)),
            pltpu.SemaphoreType.DMA((parts * slots,)),
        ],
        compiler_params=pltpu.CompilerParams(vmem_limit_bytes=VMEM_BYTES),
        cost_estimate=pl.CostEstimate(
            flops=0, bytes_accessed=4 * parts * shape.size, transcendentals=0
        ),
    )(ids, source)


def attend(query, keys, values, visible):
    rows, width = query.shape
    head_dim = width // HEADS
    bundle_width = BUNDLE * head_dim
    owner_row = lax.broadcasted_iota(jnp.int32, (BUNDLE * rows, bundle_width), 0) // rows
    owner_lane = lax.broadcasted_iota(jnp.int32, (BUNDLE * rows, bundle_width), 1) // head_dim
    own = owner_row == owner_lane
    if visible is not None:
        visible = jnp.concatenate([visible] * BUNDLE, axis=0)
    mixed = []
    for bundle in range(HEADS // BUNDLE):
        lanes = slice(bundle * bundle_width, (bundle + 1) * bundle_width)
        stacked = jnp.concatenate([query[:, lanes]] * BUNDLE, axis=0)
        stacked = jnp.where(own, stacked, jnp.zeros((), stacked.dtype))
        scores = lax.dot_general(
            stacked, keys[:, lanes], (((1,), (1,)), ((), ())), preferred_element_type=jnp.float32
        )
        if visible is not None:
            scores = jnp.where(visible, scores, NEGATIVE)
        expo = jnp.exp(scores - jnp.max(scores, axis=-1, keepdims=True))
        total = jnp.sum(expo, axis=-1, keepdims=True)
        mix = jnp.dot(
            expo.astype(jnp.bfloat16), values[:, lanes], preferred_element_type=jnp.float32
        )
        mix = jnp.where(own, mix / total, 0.0)
        folded = mix[:rows]
        for part in range(1, BUNDLE):
            folded = folded + mix[part * rows : (part + 1) * rows]
        mixed.append(folded.astype(jnp.bfloat16))
    return jnp.concatenate(mixed, axis=1)


def self_kernel(ids_ref, lens_ref, query_ref, key_ref, value_ref, reach_ref, *rest):
    page_refs, out_ref = rest[:-1], rest[-1]
    request = pl.program_id(0)
    width = query_ref.shape[1]
    rows = query_ref.shape[0]
    context = sum(ref.shape[1] for ref in page_refs)
    keys = jnp.concatenate([ref[0, :, :width] for ref in page_refs] + [key_ref[...]], axis=0)
    values = jnp.concatenate([ref[0, :, width:] for ref in page_refs] + [value_ref[...]], axis=0)
    positions = lax.broadcasted_iota(jnp.int32, (rows, context), 1)
    cached = jnp.where(positions < lens_ref[request], 1.0, 0.0)
    visible = jnp.concatenate([cached, reach_ref[0]], axis=1) > 0.5
    out_ref[...] = attend(query_ref[...], keys, values, visible)


def self_attention(query, key_new, value_new, pages, page_ids, cache_lens, reach):
    req_count, draft_len, _ = reach.shape
    width = query.shape[1]
    page_count = page_ids.shape[0] // req_count
    page_block = (1,) + pages.shape[1:]
    row_spec = pl.BlockSpec((draft_len, width), lambda n, ids, lens: (n, 0))

    def page_spec(place):
        return pl.BlockSpec(page_block, lambda n, ids, lens: (ids[n * page_count + place], 0, 0))

    keys_total = page_count * pages.shape[1] + draft_len
    return pl.pallas_call(
        self_kernel,
        grid_spec=pltpu.PrefetchScalarGridSpec(
            num_scalar_prefetch=2,
            grid=(req_count,),
            in_specs=[
                row_spec,
                row_spec,
                row_spec,
                pl.BlockSpec((1, draft_len, draft_len), lambda n, ids, lens: (n, 0, 0)),
            ]
            + [page_spec(place) for place in range(page_count)],
            out_specs=row_spec,
        ),
        out_shape=jax.ShapeDtypeStruct(query.shape, jnp.bfloat16),
        cost_estimate=pl.CostEstimate(
            flops=4 * BUNDLE * query.shape[0] * keys_total * width,
            bytes_accessed=4 * req_count * keys_total * width + 8 * query.size,
            transcendentals=query.shape[0] * keys_total * HEADS,
        ),
    )(page_ids, cache_lens, query, key_new, value_new, reach, *([pages] * page_count))


def cross_kernel(query_ref, *rest):
    memory_refs, out_ref = rest[:-1], rest[-1]
    width = query_ref.shape[1]

    def joined(lanes):
        return jnp.concatenate(
            [
                ref[0, block, :, lanes]
                for ref in memory_refs
                for block in range(ref.shape[1])
            ],
            axis=0,
        )

    out_ref[...] = attend(
        query_ref[...], joined(slice(0, width)), joined(slice(width, 2 * width)), None
    )


def cross_attention(query, memory_parts):
    req_count = memory_parts[0].shape[0]
    rows, width = query.shape
    draft_len = rows // req_count
    row_spec = pl.BlockSpec((draft_len, width), lambda n: (n, 0))
    memory_size = sum(part.size for part in memory_parts)
    return pl.pallas_call(
        cross_kernel,
        grid=(req_count,),
        in_specs=[row_spec]
        + [pl.BlockSpec((1,) + part.shape[1:], lambda n: (n, 0, 0, 0)) for part in memory_parts],
        out_specs=row_spec,
        out_shape=jax.ShapeDtypeStruct(query.shape, jnp.bfloat16),
        cost_estimate=pl.CostEstimate(
            flops=2 * BUNDLE * draft_len * memory_size,
            bytes_accessed=2 * memory_size + 4 * query.size,
            transcendentals=HEADS * draft_len * memory_size // (2 * width),
        ),
    )(query, *memory_parts)


def fetch_prompts(memory_kv):
    columns = lax.axis_size("grp")
    col_index = lax.axis_index("grp")
    share = memory_kv.shape[1] // columns
    quarter = lax.dynamic_slice_in_dim(memory_kv, col_index * share, share, 1)
    return lax.all_gather(quarter, "req", axis=0, tiled=False)


def trade_prompts(gathered, column_groups):
    columns = lax.axis_size("grp")
    col_index = lax.axis_index("grp")
    rolled = lax.dynamic_slice_in_dim(
        jnp.concatenate([column_groups, column_groups], axis=0), col_index, columns, 0
    )
    packed = take_prompts(gathered, rolled.reshape(-1), columns)
    arrived = [packed[0]]
    for shift in range(1, columns):
        ring = [(column, (column + shift) % columns) for column in range(columns)]
        arrived.append(lax.ppermute(packed[shift], "grp", ring))
    return arrived


def page_plan(page_table, pool_pages, row_index):
    owners = page_table.shape[0]
    capacity = pool_pages // owners + 1
    page_map = page_table.reshape(owners, -1)
    source = page_map // pool_pages
    slot_ids = page_map % pool_pages
    from_here = source == row_index
    send_order = jnp.cumsum(from_here.astype(jnp.int32), axis=1) - 1
    slots = jnp.arange(capacity, dtype=jnp.int32)
    placing = from_here[:, :, None] & (send_order[:, :, None] == slots[None, None, :])
    send_ids = jnp.sum(jnp.where(placing, slot_ids[:, :, None], 0), axis=1).reshape(-1)
    my_source = lax.dynamic_index_in_dim(source, row_index, 0, keepdims=False)
    page_ids = jnp.arange(page_map.shape[1], dtype=jnp.int32)
    earlier = (my_source[:, None] == my_source[None, :]) & (page_ids[None, :] < page_ids[:, None])
    page_rank = jnp.sum(earlier.astype(jnp.int32), axis=1)
    return send_ids, my_source * capacity + page_rank


def exchange(packed, owners):
    shaped = packed.reshape((owners, packed.shape[0] // owners) + packed.shape[1:])
    return lax.all_to_all(shaped, "req", split_axis=0, concat_axis=0, tiled=True)


def per_device(
    tokens,
    kv_pool,
    page_table,
    cache_lens,
    draft_lengths,
    draft_parents,
    accepted_path,
    prompt_group,
    memory_kv,
    w_query,
    w_key,
    w_value,
    w_output,
    w_cross_query,
    w_cross_output,
    w_in,
    w_out,
):
    req_count, draft_len, model_width = tokens.shape
    owners = page_table.shape[0]
    head_dim = model_width // HEADS
    scale = head_dim ** (-0.5)
    row_index = lax.axis_index("req")
    col_index = lax.axis_index("grp")
    send_ids, page_ids = page_plan(page_table, kv_pool.shape[0], row_index)
    shared = memory_kv.shape[1] // lax.axis_size("grp") >= 8
    if shared:
        column_groups = lax.all_gather(prompt_group, "grp", axis=0, tiled=False)
        send_ids, column_groups = lax.optimization_barrier((send_ids, column_groups))
        gathered = fetch_prompts(memory_kv)
        packed, w_in, w_out = lax.optimization_barrier(
            (take_blocks(kv_pool, send_ids), w_in, w_out)
        )
        pages = exchange(packed, owners)
        memory_parts = trade_prompts(gathered, column_groups)
    else:
        all_groups = lax.all_gather(prompt_group, "req", axis=0, tiled=True)
        pages = exchange(take_blocks(kv_pool, send_ids), owners)
        memory = exchange(take_blocks(memory_kv, all_groups), owners)
        memory_parts = [jnp.transpose(memory, (1, 0, 2, 3))]
    pages = pages.reshape((-1,) + kv_pool.shape[1:])
    w_in_full = lax.all_gather(w_in, "grp", axis=0, tiled=False)
    w_out_full = lax.all_gather(w_out, "grp", axis=0, tiled=True)

    flat_rows = tokens.reshape(req_count * draft_len, model_width)
    query_rows = (jnp.dot(flat_rows, w_query, preferred_element_type=jnp.float32) * scale).astype(
        jnp.bfloat16
    )
    key_new = jnp.dot(flat_rows, w_key, preferred_element_type=jnp.float32).astype(jnp.bfloat16)
    value_new = jnp.dot(flat_rows, w_value, preferred_element_type=jnp.float32).astype(jnp.bfloat16)
    reach = ancestors(draft_parents)
    path_pick = (
        accepted_path[:, :, None] == jnp.arange(draft_len, dtype=jnp.int32)[None, None, :]
    ).astype(jnp.bfloat16)
    accepted_kv = jnp.concatenate(
        [
            jnp.einsum(
                "nij,njc->nic",
                path_pick,
                part.reshape(req_count, draft_len, model_width),
                preferred_element_type=jnp.float32,
            ).astype(jnp.bfloat16)
            for part in (key_new, value_new)
        ],
        axis=2,
    )
    self_mix = self_attention(query_rows, key_new, value_new, pages, page_ids, cache_lens, reach)
    first_norm = layer_norm(
        flat_rows.astype(jnp.float32)
        + jnp.dot(self_mix, w_output, preferred_element_type=jnp.float32)
    ).astype(jnp.bfloat16)
    cross_query = (
        jnp.dot(first_norm, w_cross_query, preferred_element_type=jnp.float32) * scale
    ).astype(jnp.bfloat16)
    cross_mix = cross_attention(cross_query, memory_parts)
    second_norm = layer_norm(
        first_norm.astype(jnp.float32)
        + jnp.dot(cross_mix, w_cross_output, preferred_element_type=jnp.float32)
    ).astype(jnp.bfloat16)
    summed = jnp.zeros(second_norm.shape, jnp.float32)
    hidden = [
        jax.nn.gelu(
            jnp.dot(second_norm, w_in_full[part], preferred_element_type=jnp.float32),
            approximate=False,
        ).astype(jnp.bfloat16)
        for part in range(w_in_full.shape[0])
    ]
    summed = jnp.dot(
        jnp.concatenate(hidden, axis=1), w_out_full, preferred_element_type=jnp.float32
    )
    group_lengths = draft_lengths[0]
    own_counts = lax.dynamic_slice_in_dim(group_lengths, col_index * req_count, req_count, 0)
    live = (jnp.arange(draft_len, dtype=jnp.int32)[None, :] < own_counts[:, None]).reshape(
        req_count * draft_len
    )
    normed = layer_norm(second_norm.astype(jnp.float32) + summed).astype(jnp.bfloat16)
    result_rows = jnp.where(live[:, None], normed, jnp.zeros((), jnp.bfloat16))
    return (result_rows.reshape(req_count, draft_len, model_width), accepted_kv)


def solution(mesh):
    return jax.shard_map(
        per_device,
        mesh=mesh,
        in_specs=(
            P(("req", "grp"), None, None),
            P("req", "grp", None),
            P(None, "grp", None),
            P(("req", "grp")),
            P("req", None),
            P(("req", "grp"), None),
            P(("req", "grp"), None),
            P(("req", "grp")),
            P(None, "req", None),
            P(),
            P(),
            P(),
            P(),
            P(),
            P(),
            P(None, "grp"),
            P("grp", None),
        ),
        out_specs=(P(("req", "grp"), None, None), P(("req", "grp"), None, None)),
        check_vma=False,
    )
```

```python
import functools

import jax
import jax.numpy as jnp
from jax import lax
from jax.experimental import pallas as pl
from jax.experimental.pallas import tpu as pltpu
from jax.sharding import PartitionSpec as P

HEADS = 16
BUNDLE = 4


EPSILON = 1e-05
NEGATIVE = -1e30


def layer_norm(values):
    center = values - jnp.mean(values, axis=-1, keepdims=True)
    spread = jnp.mean(center * center, axis=-1, keepdims=True)
    return center * lax.rsqrt(spread + EPSILON)


def ancestors(parents):
    draft_len = parents.shape[-1]
    column_ids = jnp.arange(draft_len, dtype=jnp.int32)
    linked = (parents[:, :, None] == column_ids[None, None, :]).astype(jnp.float32)
    closure = linked + jnp.eye(draft_len, dtype=jnp.float32)[None]
    for sweep_index in range(draft_len.bit_length()):
        half = closure.astype(jnp.bfloat16)
        closure = jnp.minimum(
            jnp.einsum("nij,njk->nik", half, half, preferred_element_type=jnp.float32), 1.0
        )
    return closure


VMEM_BYTES = 24 * 1024 * 1024


def stream(sources, targets, held_ref, in_sems, out_sems):
    loads = [
        pltpu.make_async_copy(source, held_ref.at[slot], in_sems.at[slot])
        for slot, source in enumerate(sources)
    ]
    stores = [
        pltpu.make_async_copy(held_ref.at[slot], target, out_sems.at[slot])
        for slot, target in enumerate(targets)
    ]
    for load in loads:
        load.start()
    for load, store in zip(loads, stores):
        load.wait()
        store.start()
    for store in stores:
        store.wait()


def pack_kernel(count, ids_ref, source_ref, out_ref, held_ref, in_sems, out_sems):
    sources = [source_ref.at[ids_ref[slot]] for slot in range(count)]
    stream(sources, [out_ref.at[slot] for slot in range(count)], held_ref, in_sems, out_sems)


def take_blocks(source, ids):
    count = ids.shape[0]
    return pl.pallas_call(
        functools.partial(pack_kernel, count),
        in_specs=[
            pl.BlockSpec(memory_space=pltpu.SMEM),
            pl.BlockSpec(memory_space=pl.ANY),
        ],
        out_specs=pl.BlockSpec(memory_space=pl.ANY),
        out_shape=jax.ShapeDtypeStruct((count,) + source.shape[1:], source.dtype),
        scratch_shapes=[
            pltpu.VMEM((count,) + source.shape[1:], source.dtype),
            pltpu.SemaphoreType.DMA((count,)),
            pltpu.SemaphoreType.DMA((count,)),
        ],
        compiler_params=pltpu.CompilerParams(vmem_limit_bytes=VMEM_BYTES),
        cost_estimate=pl.CostEstimate(
            flops=0, bytes_accessed=4 * count * source[0].size, transcendentals=0
        ),
    )(ids, source)


def attend(query, keys, values, visible):
    rows, width = query.shape
    head_dim = width // HEADS
    bundle_width = BUNDLE * head_dim
    owner_row = lax.broadcasted_iota(jnp.int32, (BUNDLE * rows, bundle_width), 0) // rows
    owner_lane = lax.broadcasted_iota(jnp.int32, (BUNDLE * rows, bundle_width), 1) // head_dim
    own = owner_row == owner_lane
    if visible is not None:
        visible = jnp.concatenate([visible] * BUNDLE, axis=0)
    mixed = []
    for bundle in range(HEADS // BUNDLE):
        lanes = slice(bundle * bundle_width, (bundle + 1) * bundle_width)
        stacked = jnp.concatenate([query[:, lanes]] * BUNDLE, axis=0)
        stacked = jnp.where(own, stacked, jnp.zeros((), stacked.dtype))
        scores = lax.dot_general(
            stacked, keys[:, lanes], (((1,), (1,)), ((), ())), preferred_element_type=jnp.float32
        )
        if visible is not None:
            scores = jnp.where(visible, scores, NEGATIVE)
        expo = jnp.exp(scores - jnp.max(scores, axis=-1, keepdims=True))
        total = jnp.sum(expo, axis=-1, keepdims=True)
        mix = jnp.dot(
            expo.astype(jnp.bfloat16), values[:, lanes], preferred_element_type=jnp.float32
        )
        mix = jnp.where(own, mix / total, 0.0)
        folded = mix[:rows]
        for part in range(1, BUNDLE):
            folded = folded + mix[part * rows : (part + 1) * rows]
        mixed.append(folded.astype(jnp.bfloat16))
    return jnp.concatenate(mixed, axis=1)


def self_kernel(ids_ref, lens_ref, query_ref, key_ref, value_ref, reach_ref, *rest):
    page_refs, out_ref = rest[:-1], rest[-1]
    request = pl.program_id(0)
    width = query_ref.shape[1]
    rows = query_ref.shape[0]
    context = sum(ref.shape[1] for ref in page_refs)
    keys = jnp.concatenate([ref[0, :, :width] for ref in page_refs] + [key_ref[...]], axis=0)
    values = jnp.concatenate([ref[0, :, width:] for ref in page_refs] + [value_ref[...]], axis=0)
    positions = lax.broadcasted_iota(jnp.int32, (rows, context), 1)
    cached = jnp.where(positions < lens_ref[request], 1.0, 0.0)
    visible = jnp.concatenate([cached, reach_ref[0]], axis=1) > 0.5
    out_ref[...] = attend(query_ref[...], keys, values, visible)


def self_attention(query, key_new, value_new, pages, page_ids, cache_lens, reach):
    req_count, draft_len, _ = reach.shape
    width = query.shape[1]
    page_count = page_ids.shape[0] // req_count
    page_block = (1,) + pages.shape[1:]
    row_spec = pl.BlockSpec((draft_len, width), lambda n, ids, lens: (n, 0))

    def page_spec(place):
        return pl.BlockSpec(page_block, lambda n, ids, lens: (ids[n * page_count + place], 0, 0))

    keys_total = page_count * pages.shape[1] + draft_len
    return pl.pallas_call(
        self_kernel,
        grid_spec=pltpu.PrefetchScalarGridSpec(
            num_scalar_prefetch=2,
            grid=(req_count,),
            in_specs=[
                row_spec,
                row_spec,
                row_spec,
                pl.BlockSpec((1, draft_len, draft_len), lambda n, ids, lens: (n, 0, 0)),
            ]
            + [page_spec(place) for place in range(page_count)],
            out_specs=row_spec,
        ),
        out_shape=jax.ShapeDtypeStruct(query.shape, jnp.bfloat16),
        cost_estimate=pl.CostEstimate(
            flops=4 * BUNDLE * query.shape[0] * keys_total * width,
            bytes_accessed=4 * req_count * keys_total * width + 8 * query.size,
            transcendentals=query.shape[0] * keys_total * HEADS,
        ),
    )(page_ids, cache_lens, query, key_new, value_new, reach, *([pages] * page_count))


def cross_kernel(query_ref, memory_ref, out_ref):
    width = query_ref.shape[1]
    positions = memory_ref.shape[0] * memory_ref.shape[2]
    keys = memory_ref[:, 0, :, :width].reshape(positions, width)
    values = memory_ref[:, 0, :, width:].reshape(positions, width)
    out_ref[...] = attend(query_ref[...], keys, values, None)


def cross_attention(query, memory):
    owners, req_count, local_src, width_both = memory.shape
    rows, width = query.shape
    draft_len = rows // req_count
    row_spec = pl.BlockSpec((draft_len, width), lambda n: (n, 0))
    return pl.pallas_call(
        cross_kernel,
        grid=(req_count,),
        in_specs=[
            row_spec,
            pl.BlockSpec((owners, 1, local_src, width_both), lambda n: (0, n, 0, 0)),
        ],
        out_specs=row_spec,
        out_shape=jax.ShapeDtypeStruct(query.shape, jnp.bfloat16),
        cost_estimate=pl.CostEstimate(
            flops=4 * BUNDLE * rows * owners * local_src * width,
            bytes_accessed=2 * memory.size + 4 * query.size,
            transcendentals=rows * owners * local_src * HEADS,
        ),
    )(query, memory)


def page_plan(page_table, pool_pages, row_index):
    owners = page_table.shape[0]
    capacity = pool_pages // owners + 1
    page_map = page_table.reshape(owners, -1)
    source = page_map // pool_pages
    slot_ids = page_map % pool_pages
    from_here = source == row_index
    send_order = jnp.cumsum(from_here.astype(jnp.int32), axis=1) - 1
    slots = jnp.arange(capacity, dtype=jnp.int32)
    placing = from_here[:, :, None] & (send_order[:, :, None] == slots[None, None, :])
    send_ids = jnp.sum(jnp.where(placing, slot_ids[:, :, None], 0), axis=1).reshape(-1)
    my_source = lax.dynamic_index_in_dim(source, row_index, 0, keepdims=False)
    page_ids = jnp.arange(page_map.shape[1], dtype=jnp.int32)
    earlier = (my_source[:, None] == my_source[None, :]) & (page_ids[None, :] < page_ids[:, None])
    page_rank = jnp.sum(earlier.astype(jnp.int32), axis=1)
    return send_ids, my_source * capacity + page_rank


def exchange(packed, owners):
    shaped = packed.reshape((owners, packed.shape[0] // owners) + packed.shape[1:])
    return lax.all_to_all(shaped, "req", split_axis=0, concat_axis=0, tiled=True)


def per_device(
    tokens,
    kv_pool,
    page_table,
    cache_lens,
    draft_lengths,
    draft_parents,
    accepted_path,
    prompt_group,
    memory_kv,
    w_query,
    w_key,
    w_value,
    w_output,
    w_cross_query,
    w_cross_output,
    w_in,
    w_out,
):
    req_count, draft_len, model_width = tokens.shape
    owners = page_table.shape[0]
    head_dim = model_width // HEADS
    scale = head_dim ** (-0.5)
    row_index = lax.axis_index("req")
    col_index = lax.axis_index("grp")
    send_ids, page_ids = page_plan(page_table, kv_pool.shape[0], row_index)
    all_groups = lax.all_gather(prompt_group, "req", axis=0, tiled=True)
    send_ids, all_groups = lax.optimization_barrier((send_ids, all_groups))
    pages = exchange(take_blocks(kv_pool, send_ids), owners)
    memory = exchange(take_blocks(memory_kv, all_groups), owners)
    pages = pages.reshape((-1,) + kv_pool.shape[1:])
    w_in_full = lax.all_gather(w_in, "grp", axis=0, tiled=False)
    w_out_full = lax.all_gather(w_out, "grp", axis=0, tiled=True)

    flat_rows = tokens.reshape(req_count * draft_len, model_width)
    query_rows = (jnp.dot(flat_rows, w_query, preferred_element_type=jnp.float32) * scale).astype(
        jnp.bfloat16
    )
    key_new = jnp.dot(flat_rows, w_key, preferred_element_type=jnp.float32).astype(jnp.bfloat16)
    value_new = jnp.dot(flat_rows, w_value, preferred_element_type=jnp.float32).astype(jnp.bfloat16)
    reach = ancestors(draft_parents)
    path_pick = (
        accepted_path[:, :, None] == jnp.arange(draft_len, dtype=jnp.int32)[None, None, :]
    ).astype(jnp.bfloat16)
    accepted_kv = jnp.concatenate(
        [
            jnp.einsum(
                "nij,njc->nic",
                path_pick,
                part.reshape(req_count, draft_len, model_width),
                preferred_element_type=jnp.float32,
            ).astype(jnp.bfloat16)
            for part in (key_new, value_new)
        ],
        axis=2,
    )
    self_mix = self_attention(query_rows, key_new, value_new, pages, page_ids, cache_lens, reach)
    first_norm = layer_norm(
        flat_rows.astype(jnp.float32)
        + jnp.dot(self_mix, w_output, preferred_element_type=jnp.float32)
    ).astype(jnp.bfloat16)
    cross_query = (
        jnp.dot(first_norm, w_cross_query, preferred_element_type=jnp.float32) * scale
    ).astype(jnp.bfloat16)
    cross_mix = cross_attention(cross_query, memory)
    second_norm = layer_norm(
        first_norm.astype(jnp.float32)
        + jnp.dot(cross_mix, w_cross_output, preferred_element_type=jnp.float32)
    ).astype(jnp.bfloat16)
    summed = jnp.zeros(second_norm.shape, jnp.float32)
    hidden = [
        jax.nn.gelu(
            jnp.dot(second_norm, w_in_full[part], preferred_element_type=jnp.float32),
            approximate=False,
        ).astype(jnp.bfloat16)
        for part in range(w_in_full.shape[0])
    ]
    summed = jnp.dot(
        jnp.concatenate(hidden, axis=1), w_out_full, preferred_element_type=jnp.float32
    )
    group_lengths = draft_lengths[0]
    own_counts = lax.dynamic_slice_in_dim(group_lengths, col_index * req_count, req_count, 0)
    live = (jnp.arange(draft_len, dtype=jnp.int32)[None, :] < own_counts[:, None]).reshape(
        req_count * draft_len
    )
    normed = layer_norm(second_norm.astype(jnp.float32) + summed).astype(jnp.bfloat16)
    result_rows = jnp.where(live[:, None], normed, jnp.zeros((), jnp.bfloat16))
    return (result_rows.reshape(req_count, draft_len, model_width), accepted_kv)


def solution(mesh):
    return jax.shard_map(
        per_device,
        mesh=mesh,
        in_specs=(
            P(("req", "grp"), None, None),
            P("req", "grp", None),
            P(None, "grp", None),
            P(("req", "grp")),
            P("req", None),
            P(("req", "grp"), None),
            P(("req", "grp"), None),
            P(("req", "grp")),
            P(None, "req", None),
            P(),
            P(),
            P(),
            P(),
            P(),
            P(),
            P(None, "grp"),
            P("grp", None),
        ),
        out_specs=(P(("req", "grp"), None, None), P(("req", "grp"), None, None)),
        check_vma=False,
    )
```

```python
import functools

import jax
import jax.numpy as jnp
from jax import lax
from jax.experimental import pallas as pl
from jax.experimental.pallas import tpu as pltpu
from jax.sharding import PartitionSpec as P

HEADS = 16
BUNDLE = 4


EPSILON = 1e-05
NEGATIVE = -1e30


def layer_norm(values):
    center = values - jnp.mean(values, axis=-1, keepdims=True)
    spread = jnp.mean(center * center, axis=-1, keepdims=True)
    return center * lax.rsqrt(spread + EPSILON)


def ancestors(parents):
    draft_len = parents.shape[-1]
    column_ids = jnp.arange(draft_len, dtype=jnp.int32)
    linked = (parents[:, :, None] == column_ids[None, None, :]).astype(jnp.float32)
    closure = linked + jnp.eye(draft_len, dtype=jnp.float32)[None]
    for sweep_index in range(draft_len.bit_length()):
        half = closure.astype(jnp.bfloat16)
        closure = jnp.minimum(
            jnp.einsum("nij,njk->nik", half, half, preferred_element_type=jnp.float32), 1.0
        )
    return closure


VMEM_BYTES = 24 * 1024 * 1024


def stream(sources, targets, held_ref, in_sems, out_sems):
    loads = [
        pltpu.make_async_copy(source, held_ref.at[slot], in_sems.at[slot])
        for slot, source in enumerate(sources)
    ]
    stores = [
        pltpu.make_async_copy(held_ref.at[slot], target, out_sems.at[slot])
        for slot, target in enumerate(targets)
    ]
    for load in loads:
        load.start()
    for load, store in zip(loads, stores):
        load.wait()
        store.start()
    for store in stores:
        store.wait()


def pack_kernel(count, ids_ref, source_ref, out_ref, held_ref, in_sems, out_sems):
    sources = [source_ref.at[ids_ref[slot]] for slot in range(count)]
    stream(sources, [out_ref.at[slot] for slot in range(count)], held_ref, in_sems, out_sems)


def take_blocks(source, ids):
    count = ids.shape[0]
    return pl.pallas_call(
        functools.partial(pack_kernel, count),
        in_specs=[
            pl.BlockSpec(memory_space=pltpu.SMEM),
            pl.BlockSpec(memory_space=pl.ANY),
        ],
        out_specs=pl.BlockSpec(memory_space=pl.ANY),
        out_shape=jax.ShapeDtypeStruct((count,) + source.shape[1:], source.dtype),
        scratch_shapes=[
            pltpu.VMEM((count,) + source.shape[1:], source.dtype),
            pltpu.SemaphoreType.DMA((count,)),
            pltpu.SemaphoreType.DMA((count,)),
        ],
        compiler_params=pltpu.CompilerParams(vmem_limit_bytes=VMEM_BYTES),
        cost_estimate=pl.CostEstimate(
            flops=0, bytes_accessed=4 * count * source[0].size, transcendentals=0
        ),
    )(ids, source)


def attend(query, keys, values, visible):
    rows, width = query.shape
    head_dim = width // HEADS
    bundle_width = BUNDLE * head_dim
    owner_row = lax.broadcasted_iota(jnp.int32, (BUNDLE * rows, bundle_width), 0) // rows
    owner_lane = lax.broadcasted_iota(jnp.int32, (BUNDLE * rows, bundle_width), 1) // head_dim
    own = owner_row == owner_lane
    if visible is not None:
        visible = jnp.concatenate([visible] * BUNDLE, axis=0)
    mixed = []
    for bundle in range(HEADS // BUNDLE):
        lanes = slice(bundle * bundle_width, (bundle + 1) * bundle_width)
        stacked = jnp.concatenate([query[:, lanes]] * BUNDLE, axis=0)
        stacked = jnp.where(own, stacked, jnp.zeros((), stacked.dtype))
        scores = lax.dot_general(
            stacked, keys[:, lanes], (((1,), (1,)), ((), ())), preferred_element_type=jnp.float32
        )
        if visible is not None:
            scores = jnp.where(visible, scores, NEGATIVE)
        expo = jnp.exp(scores - jnp.max(scores, axis=-1, keepdims=True))
        total = jnp.sum(expo, axis=-1, keepdims=True)
        mix = jnp.dot(
            expo.astype(jnp.bfloat16), values[:, lanes], preferred_element_type=jnp.float32
        )
        mix = jnp.where(own, mix / total, 0.0)
        folded = mix[:rows]
        for part in range(1, BUNDLE):
            folded = folded + mix[part * rows : (part + 1) * rows]
        mixed.append(folded.astype(jnp.bfloat16))
    return jnp.concatenate(mixed, axis=1)


def self_kernel(ids_ref, lens_ref, query_ref, key_ref, value_ref, reach_ref, *rest):
    page_refs, out_ref = rest[:-1], rest[-1]
    request = pl.program_id(0)
    width = query_ref.shape[1]
    rows = query_ref.shape[0]
    context = sum(ref.shape[1] for ref in page_refs)
    keys = jnp.concatenate([ref[0, :, :width] for ref in page_refs] + [key_ref[...]], axis=0)
    values = jnp.concatenate([ref[0, :, width:] for ref in page_refs] + [value_ref[...]], axis=0)
    positions = lax.broadcasted_iota(jnp.int32, (rows, context), 1)
    cached = jnp.where(positions < lens_ref[request], 1.0, 0.0)
    visible = jnp.concatenate([cached, reach_ref[0]], axis=1) > 0.5
    out_ref[...] = attend(query_ref[...], keys, values, visible)


def self_attention(query, key_new, value_new, pages, page_ids, cache_lens, reach):
    req_count, draft_len, _ = reach.shape
    width = query.shape[1]
    page_count = page_ids.shape[0] // req_count
    page_block = (1,) + pages.shape[1:]
    row_spec = pl.BlockSpec((draft_len, width), lambda n, ids, lens: (n, 0))

    def page_spec(place):
        return pl.BlockSpec(page_block, lambda n, ids, lens: (ids[n * page_count + place], 0, 0))

    keys_total = page_count * pages.shape[1] + draft_len
    return pl.pallas_call(
        self_kernel,
        grid_spec=pltpu.PrefetchScalarGridSpec(
            num_scalar_prefetch=2,
            grid=(req_count,),
            in_specs=[
                row_spec,
                row_spec,
                row_spec,
                pl.BlockSpec((1, draft_len, draft_len), lambda n, ids, lens: (n, 0, 0)),
            ]
            + [page_spec(place) for place in range(page_count)],
            out_specs=row_spec,
        ),
        out_shape=jax.ShapeDtypeStruct(query.shape, jnp.bfloat16),
        cost_estimate=pl.CostEstimate(
            flops=4 * BUNDLE * query.shape[0] * keys_total * width,
            bytes_accessed=4 * req_count * keys_total * width + 8 * query.size,
            transcendentals=query.shape[0] * keys_total * HEADS,
        ),
    )(page_ids, cache_lens, query, key_new, value_new, reach, *([pages] * page_count))


def cross_kernel(query_ref, memory_ref, out_ref):
    width = query_ref.shape[1]
    positions = memory_ref.shape[0] * memory_ref.shape[2]
    keys = memory_ref[:, 0, :, :width].reshape(positions, width)
    values = memory_ref[:, 0, :, width:].reshape(positions, width)
    out_ref[...] = attend(query_ref[...], keys, values, None)


def cross_attention(query, memory):
    owners, req_count, local_src, width_both = memory.shape
    rows, width = query.shape
    draft_len = rows // req_count
    row_spec = pl.BlockSpec((draft_len, width), lambda n: (n, 0))
    return pl.pallas_call(
        cross_kernel,
        grid=(req_count,),
        in_specs=[
            row_spec,
            pl.BlockSpec((owners, 1, local_src, width_both), lambda n: (0, n, 0, 0)),
        ],
        out_specs=row_spec,
        out_shape=jax.ShapeDtypeStruct(query.shape, jnp.bfloat16),
        cost_estimate=pl.CostEstimate(
            flops=4 * BUNDLE * rows * owners * local_src * width,
            bytes_accessed=2 * memory.size + 4 * query.size,
            transcendentals=rows * owners * local_src * HEADS,
        ),
    )(query, memory)


def page_plan(page_table, pool_pages, row_index):
    owners = page_table.shape[0]
    capacity = pool_pages // owners + 1
    page_map = page_table.reshape(owners, -1)
    source = page_map // pool_pages
    slot_ids = page_map % pool_pages
    from_here = source == row_index
    send_order = jnp.cumsum(from_here.astype(jnp.int32), axis=1) - 1
    slots = jnp.arange(capacity, dtype=jnp.int32)
    placing = from_here[:, :, None] & (send_order[:, :, None] == slots[None, None, :])
    send_ids = jnp.sum(jnp.where(placing, slot_ids[:, :, None], 0), axis=1).reshape(-1)
    my_source = lax.dynamic_index_in_dim(source, row_index, 0, keepdims=False)
    page_ids = jnp.arange(page_map.shape[1], dtype=jnp.int32)
    earlier = (my_source[:, None] == my_source[None, :]) & (page_ids[None, :] < page_ids[:, None])
    page_rank = jnp.sum(earlier.astype(jnp.int32), axis=1)
    return send_ids, my_source * capacity + page_rank


def exchange(packed, owners):
    shaped = packed.reshape((owners, packed.shape[0] // owners) + packed.shape[1:])
    return lax.all_to_all(shaped, "req", split_axis=0, concat_axis=0, tiled=True)


def per_device(
    tokens,
    kv_pool,
    page_table,
    cache_lens,
    draft_lengths,
    draft_parents,
    accepted_path,
    prompt_group,
    memory_kv,
    w_query,
    w_key,
    w_value,
    w_output,
    w_cross_query,
    w_cross_output,
    w_in,
    w_out,
):
    req_count, draft_len, model_width = tokens.shape
    owners = page_table.shape[0]
    head_dim = model_width // HEADS
    scale = head_dim ** (-0.5)
    row_index = lax.axis_index("req")
    col_index = lax.axis_index("grp")
    send_ids, page_ids = page_plan(page_table, kv_pool.shape[0], row_index)
    all_groups = lax.all_gather(prompt_group, "req", axis=0, tiled=True)
    send_ids, all_groups = lax.optimization_barrier((send_ids, all_groups))
    pages = exchange(take_blocks(kv_pool, send_ids), owners)
    memory = exchange(take_blocks(memory_kv, all_groups), owners)
    pages = pages.reshape((-1,) + kv_pool.shape[1:])
    w_in_full = lax.all_gather(w_in, "grp", axis=1, tiled=True)
    w_out_full = lax.all_gather(w_out, "grp", axis=0, tiled=True)

    flat_rows = tokens.reshape(req_count * draft_len, model_width)
    query_rows = (jnp.dot(flat_rows, w_query, preferred_element_type=jnp.float32) * scale).astype(
        jnp.bfloat16
    )
    key_new = jnp.dot(flat_rows, w_key, preferred_element_type=jnp.float32).astype(jnp.bfloat16)
    value_new = jnp.dot(flat_rows, w_value, preferred_element_type=jnp.float32).astype(jnp.bfloat16)
    reach = ancestors(draft_parents)
    path_pick = (
        accepted_path[:, :, None] == jnp.arange(draft_len, dtype=jnp.int32)[None, None, :]
    ).astype(jnp.bfloat16)
    accepted_kv = jnp.concatenate(
        [
            jnp.einsum(
                "nij,njc->nic",
                path_pick,
                part.reshape(req_count, draft_len, model_width),
                preferred_element_type=jnp.float32,
            ).astype(jnp.bfloat16)
            for part in (key_new, value_new)
        ],
        axis=2,
    )
    self_mix = self_attention(query_rows, key_new, value_new, pages, page_ids, cache_lens, reach)
    first_norm = layer_norm(
        flat_rows.astype(jnp.float32)
        + jnp.dot(self_mix, w_output, preferred_element_type=jnp.float32)
    ).astype(jnp.bfloat16)
    cross_query = (
        jnp.dot(first_norm, w_cross_query, preferred_element_type=jnp.float32) * scale
    ).astype(jnp.bfloat16)
    cross_mix = cross_attention(cross_query, memory)
    second_norm = layer_norm(
        first_norm.astype(jnp.float32)
        + jnp.dot(cross_mix, w_cross_output, preferred_element_type=jnp.float32)
    ).astype(jnp.bfloat16)
    hidden = jax.nn.gelu(
        jnp.dot(second_norm, w_in_full, preferred_element_type=jnp.float32), approximate=False
    ).astype(jnp.bfloat16)
    summed = jnp.dot(hidden, w_out_full, preferred_element_type=jnp.float32)
    group_lengths = draft_lengths[0]
    own_counts = lax.dynamic_slice_in_dim(group_lengths, col_index * req_count, req_count, 0)
    live = (jnp.arange(draft_len, dtype=jnp.int32)[None, :] < own_counts[:, None]).reshape(
        req_count * draft_len
    )
    normed = layer_norm(second_norm.astype(jnp.float32) + summed).astype(jnp.bfloat16)
    result_rows = jnp.where(live[:, None], normed, jnp.zeros((), jnp.bfloat16))
    return (result_rows.reshape(req_count, draft_len, model_width), accepted_kv)


def solution(mesh):
    return jax.shard_map(
        per_device,
        mesh=mesh,
        in_specs=(
            P(("req", "grp"), None, None),
            P("req", "grp", None),
            P(None, "grp", None),
            P(("req", "grp")),
            P("req", None),
            P(("req", "grp"), None),
            P(("req", "grp"), None),
            P(("req", "grp")),
            P(None, "req", None),
            P(),
            P(),
            P(),
            P(),
            P(),
            P(),
            P(None, "grp"),
            P("grp", None),
        ),
        out_specs=(P(("req", "grp"), None, None), P(("req", "grp"), None, None)),
        check_vma=False,
    )
```
